32 devices in a mesh: geom: 2 (over x), pair: 16 (over z, y, core).
Axes of the slice: x: 2, y: 2, z: 4, core: 2. Of those that a mesh axis runs over, the one named last changes fastest.
Arguments:
- walkers: float32 [32, 64, 512], P(('geom', 'pair')), parts along dimension 0, may hold values from -6 to 6
- cholesky: bfloat16 [10240, 256, 513], P('geom', 'pair'), parts along dimension 0, may hold values from -0.33663118 to 0.33663118
- field_seeds: int32 [5120, 32], P('pair', 'geom'), parts along dimension 1, may hold values from 0 to 131071
- slot_order: int32 [32], P('geom'), parts along dimension 0, may hold values from 0 to 15, each once
Outputs:
- moved: float32 [32, 64, 512], P(('geom', 'pair')), parts along dimension 0
- log_weights: float32 [32], P(('geom', 'pair')), parts along dimension 0
The draws below stay inside these ranges and needn't reach their ends.
There are 2 independent parts, one for each index of `geom`. The reference program is written for one: setup_inputs(seed, part) draws one part's arguments, and reference() takes and returns one part's arrays. A program takes and returns all parts, laid end to end along the dimension named above; each array names one. Nothing has to cross between parts.
Inputs may be any that keep to these rules, and one draw needn't show every extreme that they name: `slot_order`: a permutation of the walker numbers.
All inputs are finite; a program needn't handle non-finite values.
Results may differ from the reference program's by a relative error of at most 0.0044.
Values may be sent and summed in bfloat16 or wider, within the bound.
A program may use at most 320 MiB of HBM per device.

```python
import math
import jax
import jax.numpy as jnp
from jax import lax

M = 512
NOCC = 64
NCHOL = 5120
WALKERS = 16
ROWS_DEV = 16
CHOL_DEV = 320


def draw_walkers(key, part):
    key_values, key_region = jax.random.split(jax.random.fold_in(key, 4242), 2)
    array_shape = (WALKERS, NOCC, M)
    values = jax.random.truncated_normal(key_values, -6.0, 6.0, array_shape, jnp.float32)
    region = jax.random.randint(key_region, (WALKERS,), 0, 4)
    orbital_region = jnp.arange(M) // (M // 4)
    inside = orbital_region[None, :] == region[:, None]
    column_scale = jnp.where(inside, 1.0, 0.15)
    return values * column_scale[:, None, :]


def draw_cholesky(key, part):
    key_base, key_spike, key_offset, key_factor = jax.random.split(key, 4)
    noise_scale = 6.0 / (M * NCHOL) ** 0.5
    offset_scale = 0.52 / NOCC
    array_shape = (NCHOL, M // 2, M + 1)
    random_part = jax.random.truncated_normal(key_base, -6.0, 6.0, array_shape, jnp.float32)
    offsets = jax.random.truncated_normal(key_offset, -4.0, 4.0, (NCHOL,), jnp.float32)
    blocks = M // 2 // ROWS_DEV
    partner = jax.random.permutation(key_spike, blocks)
    row_block = jnp.arange(M // 2) // ROWS_DEV
    chol_block = jnp.arange(NCHOL) // CHOL_DEV
    spiked = partner[row_block][None, :, None] == chol_block[:, None, None]
    folded_row = jnp.arange(M // 2)[:, None]
    folded_col = jnp.arange(M + 1)[None, :]
    first_half = folded_col < M - folded_row
    row_orbital = jnp.where(first_half, folded_row, M - 1 - folded_row)
    col_orbital = jnp.where(first_half, folded_row + folded_col, 2 * M - 1 - folded_row - folded_col)
    same_region = row_orbital // (M // 4) == col_orbital // (M // 4)
    region_scale = jnp.where(same_region, 2.2, 0.35)
    random_part = random_part * jnp.where(spiked, 4.0, 1.0) * region_scale[None, :, :] * noise_scale
    factor = jnp.exp(jax.random.uniform(key_factor, (NCHOL, M // 2, 2), jnp.float32, math.log(0.25), math.log(4.0)))
    diagonal = (offset_scale * offsets)[:, None, None] * factor
    column = jnp.arange(M + 1)[None, None, :]
    additions = jnp.where(column == 0, diagonal[:, :, 0:1], 0.0) + jnp.where(column == M, diagonal[:, :, 1:2], 0.0)
    return (random_part + additions).astype(jnp.bfloat16)


def touch_ends(values, own_key, least, top_value):
    longest = values.shape.index(max(values.shape))
    spots = []
    for shift in (0, 1):
        where = [jax.random.randint(jax.random.fold_in(own_key, axis), (), 0, length) for axis, length in enumerate(values.shape)]
        where[longest] = (where[longest] + shift) % values.shape[longest]
        spots.append(tuple(where))
    return values.at[spots[0]].set(least).at[spots[1]].set(top_value)


def setup_inputs(seed: int = 0, part: int = 0) -> dict:
    key_of = jax.random.split(jax.random.key(seed), 5)
    part_keys = jax.random.split(jax.random.fold_in(key_of[4], part), 5)
    walkers = draw_walkers(jax.random.fold_in(jax.random.fold_in(key_of[4], part), 71), part)
    cholesky = draw_cholesky(jax.random.fold_in(jax.random.fold_in(key_of[4], part), 71), part)
    field_seeds = touch_ends(jax.random.randint(part_keys[2], (NCHOL, WALKERS), 0, 131072), jax.random.fold_in(part_keys[2], 1), 0, 131071).astype(jnp.int32)
    slot_order = jax.random.permutation(part_keys[3], WALKERS).astype(jnp.int32)
    return {"walkers": walkers, "cholesky": cholesky, "field_seeds": field_seeds, "slot_order": slot_order}


sqrt_step = 0.1

def pair_weights(orbits):
    column = jnp.arange(orbits + 1)
    return jnp.where((column == 0) | (column == orbits), 1.0, 2.0).astype(jnp.float32)

def skew_left(rows, start, width):
    count = rows.shape[-2]
    span = rows.shape[-1]
    lead = rows.shape[:-2]
    flat = rows.reshape(lead + (count * span,))
    flat = jnp.concatenate([flat, jnp.zeros(lead + (count + span,), rows.dtype)], axis=-1)
    window = lax.dynamic_slice_in_dim(flat, start, count * (span + 1), len(lead))
    return window.reshape(lead + (count, span + 1))[..., :width]

def fold_rows(upper_rows, lower_rows, start):
    orbits = upper_rows.shape[-1]
    joined = jnp.concatenate([upper_rows.astype(jnp.float32), lower_rows.astype(jnp.float32)], axis=-1)
    return skew_left(joined, start, orbits + 1) * pair_weights(orbits)

def unfold_rows(packed):
    halfway = packed.shape[0]
    orbits = packed.shape[1] - 1
    width = 3 * orbits
    padded = jnp.concatenate([jnp.zeros((halfway, orbits), packed.dtype), packed, jnp.zeros((halfway, orbits - 1), packed.dtype)], axis=1)
    flat = jnp.concatenate([padded.reshape(-1), jnp.zeros((orbits,), packed.dtype)])
    spread = flat[orbits:orbits + halfway * (width - 1)].reshape(halfway, width - 1)[:, :2 * orbits]
    upper = jnp.concatenate([spread[:, :orbits], spread[:, orbits:][:, ::-1][::-1]], axis=0)
    return upper + upper.T - jnp.diag(jnp.diag(upper))

def density(orbital_matrix):
    intersection = jnp.dot(orbital_matrix, orbital_matrix.T, precision=lax.Precision.HIGHEST)
    factor = jnp.linalg.cholesky(intersection)
    rotated = lax.linalg.triangular_solve(factor, orbital_matrix, left_side=True, lower=True)
    return jnp.dot(rotated.T, rotated, precision=lax.Precision.HIGHEST)

def gaussian(seed_values):
    first = (seed_values % 65521 * 7919 + 13) % 65521
    second = (seed_values // 2 * 3037 + 101) % 65521
    uniform_one = (first.astype(jnp.float32) + 0.5) / 65521.0
    uniform_two = (second.astype(jnp.float32) + 0.5) / 65521.0
    return jnp.sqrt(-2.0 * jnp.log(uniform_one)) * jnp.cos(2.0 * math.pi * uniform_two)

def propagate(packed_potential, orbital_matrix):
    potential = unfold_rows(packed_potential)
    result = orbital_matrix
    term = orbital_matrix
    for degree in range(1, 7):
        term = jnp.dot(term, potential, precision=lax.Precision.HIGHEST) / degree
        result = result + term
    return result

def reference(walkers, cholesky, field_seeds, slot_order):
    orbits = walkers.shape[2]
    halfway = orbits // 2
    walk_total = walkers.shape[0]
    chol_total = cholesky.shape[0]

    def pack_one(orbital_matrix):
        green = density(orbital_matrix)
        lower_half = green[halfway:][::-1, ::-1]
        return fold_rows(green[:halfway], lower_half, 0).astype(jnp.bfloat16)
    packed = lax.map(pack_one, walkers).reshape(walk_total, -1)
    flat_chol = cholesky.reshape(chol_total, -1)
    bias = sqrt_step * lax.dot_general(flat_chol.astype(jnp.float32), packed.astype(jnp.float32), (((1,), (1,)), ((), ())), preferred_element_type=jnp.float32)
    noise = gaussian(field_seeds[:, slot_order])
    shifted = (noise - bias).astype(jnp.bfloat16)
    log_weights = lax.optimization_barrier(jnp.sum(noise * bias - 0.5 * bias * bias, axis=0))
    potential = sqrt_step * lax.dot_general(shifted.astype(jnp.float32), flat_chol.astype(jnp.float32), (((0,), (0,)), ((), ())), preferred_element_type=jnp.float32)
    potential = potential.reshape(walk_total, halfway, orbits + 1)
    moved = lax.map(lambda pieces: propagate(pieces[0], pieces[1]), (potential, walkers))
    return (moved, log_weights)
```

```python
import math

import jax
import jax.numpy as jnp
from jax import lax
from jax.experimental import pallas as pl
from jax.experimental.pallas import tpu as pltpu
from jax.sharding import PartitionSpec as P

sqrt_step = 0.1
VMEM = pl.BlockSpec(memory_space=pltpu.VMEM)


def flip_matrix(size):
    row = lax.broadcasted_iota(jnp.int32, (size, size), 0)
    col = lax.broadcasted_iota(jnp.int32, (size, size), 1)
    return jnp.where(row + col == size - 1, 1.0, 0.0).astype(jnp.bfloat16)


def exact_dot(a, b):
    return jnp.dot(a, b, preferred_element_type=jnp.float32)


def fold_kernel(green_ref, out_ref):
    orbits = green_ref.shape[0]
    halfway = orbits // 2
    flip_half = flip_matrix(halfway)
    upper = exact_dot(flip_half, green_ref[:halfway, :])
    lower = exact_dot(green_ref[halfway:, :], flip_matrix(orbits))
    joined = jnp.concatenate([upper, lower], axis=1)
    rolled = pltpu.roll(joined, orbits + halfway + 1, 1, stride=1, stride_axis=0)
    column = lax.broadcasted_iota(jnp.int32, (halfway, 2 * orbits), 1)
    weighted = jnp.where((column == 0) | (column == orbits), rolled, 2.0 * rolled)
    ordered = exact_dot(flip_half, weighted.astype(jnp.bfloat16))
    out_ref[...] = ordered[:, : orbits + 1].astype(jnp.bfloat16)


def fold(green):
    orbits = green.shape[0]
    return pl.pallas_call(
        fold_kernel,
        out_shape=jax.ShapeDtypeStruct((orbits // 2, orbits + 1), jnp.bfloat16),
        in_specs=[VMEM],
        out_specs=VMEM,
        name="fold",
    )(green)


def propagate_kernel(packed_ref, orbital_ref, out_ref):
    halfway, width = packed_ref.shape
    orbits = width - 1
    packed = packed_ref[...].astype(jnp.float32)
    padded = jnp.concatenate(
        [packed, jnp.zeros((halfway, 2 * orbits - width), jnp.float32)], axis=1
    )
    spread = pltpu.roll(padded, 0, 1, stride=1, stride_axis=0)
    backward = spread[:, orbits:].astype(jnp.bfloat16)
    turned = exact_dot(flip_matrix(halfway), backward).astype(jnp.bfloat16)
    lower = exact_dot(turned, flip_matrix(orbits))
    upper = jnp.concatenate([spread[:, :orbits], lower], axis=0)
    row = lax.broadcasted_iota(jnp.int32, (orbits, orbits), 0)
    col = lax.broadcasted_iota(jnp.int32, (orbits, orbits), 1)
    potential = jnp.where(col >= row, upper, upper.T).astype(jnp.bfloat16)
    term = orbital_ref[...]
    count = term.shape[0]
    result = term
    for degree in range(1, 7):
        high = term.astype(jnp.bfloat16)
        rest = term - high.astype(jnp.float32)
        middle = rest.astype(jnp.bfloat16)
        low = (rest - middle.astype(jnp.float32)).astype(jnp.bfloat16)
        product = exact_dot(jnp.concatenate([high, middle, low], axis=0), potential)
        term = (
            product[2 * count :] + product[count : 2 * count] + product[:count]
        ) * (1.0 / degree)
        result = result + term
    out_ref[...] = result


def propagate(packed_potential, orbital_matrix):
    return pl.pallas_call(
        propagate_kernel,
        out_shape=jax.ShapeDtypeStruct(orbital_matrix.shape, jnp.float32),
        in_specs=[VMEM, VMEM],
        out_specs=VMEM,
        name="propagate",
    )(packed_potential, orbital_matrix)


def meet_everyone(devices, own):
    barrier = pltpu.get_barrier_semaphore()

    def greet(step, carry):
        peer = lax.rem(own + step, devices)
        pl.semaphore_signal(
            barrier, inc=1, device_id={"pair": peer}, device_id_type=pl.DeviceIdType.MESH
        )
        return carry

    lax.fori_loop(1, devices, greet, 0)
    pl.semaphore_wait(barrier, devices - 1)


def remote(source, target, send_sem, recv_sem, step, peer):
    return pltpu.make_async_remote_copy(
        src_ref=source,
        dst_ref=target,
        send_sem=send_sem.at[step],
        recv_sem=recv_sem.at[step],
        device_id={"pair": peer},
        device_id_type=pl.DeviceIdType.MESH,
    )


def exchange_kernel(devices, in_ref, out_ref, send_sem, recv_sem, local_sem):
    own = lax.axis_index("pair")
    local = pltpu.make_async_copy(in_ref.at[own], out_ref.at[own], local_sem)
    local.start()
    meet_everyone(devices, own)

    def start(step, carry):
        peer = lax.rem(own + step, devices)
        remote(in_ref.at[peer], out_ref.at[own], send_sem, recv_sem, step, peer).start()
        return carry

    def finish(step, carry):
        peer = lax.rem(own + step, devices)
        source = lax.rem(own + devices - step, devices)
        remote(in_ref.at[peer], out_ref.at[source], send_sem, recv_sem, step, peer).wait()
        return carry

    lax.fori_loop(1, devices, start, 0)
    lax.fori_loop(1, devices, finish, 0)
    local.wait()


def exchange(blocks, devices, collective_id, name):
    return pl.pallas_call(
        lambda *refs: exchange_kernel(devices, *refs),
        out_shape=jax.ShapeDtypeStruct(blocks.shape, blocks.dtype),
        in_specs=[VMEM],
        out_specs=VMEM,
        scratch_shapes=[
            pltpu.SemaphoreType.DMA((devices,)),
            pltpu.SemaphoreType.DMA((devices,)),
            pltpu.SemaphoreType.DMA,
        ],
        compiler_params=pltpu.CompilerParams(
            collective_id=collective_id, has_side_effects=True
        ),
        name=name,
    )(blocks)


def fields_kernel(
    devices, partial_ref, noise_ref, shifted_ref, log_ref,
    arrived, own_shifted, own_log, all_log,
    bias_send, bias_recv, field_send, field_recv, log_send, log_recv,
):
    own = lax.axis_index("pair")
    meet_everyone(devices, own)

    def bias_copy(step, slot):
        peer = lax.rem(own + step, devices)
        return remote(partial_ref.at[peer], arrived.at[slot], bias_send, bias_recv, step, peer)

    def field_copy(step, slot):
        peer = lax.rem(own + step, devices)
        return remote(own_shifted, shifted_ref.at[slot], field_send, field_recv, step, peer)

    def log_copy(step, slot):
        peer = lax.rem(own + step, devices)
        return remote(own_log, all_log.at[slot], log_send, log_recv, step, peer)

    def start_bias(step, carry):
        bias_copy(step, own).start()
        return carry

    def finish_bias(step, total):
        source = lax.rem(own + devices - step, devices)
        bias_copy(step, source).wait()
        return total + arrived[source]

    lax.fori_loop(1, devices, start_bias, 0)
    bias = sqrt_step * lax.fori_loop(1, devices, finish_bias, partial_ref[own])
    noise = noise_ref[...]
    shifted = (noise - bias).astype(jnp.bfloat16)
    own_shifted[...] = shifted
    terms = jnp.sum(noise * bias - 0.5 * bias * bias, axis=1, keepdims=True)
    terms = jnp.broadcast_to(terms, own_log.shape)
    own_log[...] = terms

    def start_fields(step, carry):
        field_copy(step, own).start()
        return carry

    def start_logs(step, carry):
        log_copy(step, own).start()
        return carry

    def finish_fields(step, carry):
        source = lax.rem(own + devices - step, devices)
        field_copy(step, source).wait()
        return carry

    def finish_logs(step, total):
        source = lax.rem(own + devices - step, devices)
        log_copy(step, source).wait()
        return total + all_log[source]

    lax.fori_loop(1, devices, start_fields, 0)
    lax.fori_loop(1, devices, start_logs, 0)
    shifted_ref[own] = shifted
    lax.fori_loop(1, devices, finish_fields, 0)
    log_ref[...] = lax.fori_loop(1, devices, finish_logs, terms)


def fields(partial_bias, noise, devices):
    walk_total, chol_local = noise.shape
    sems = pltpu.SemaphoreType.DMA((devices,))
    return pl.pallas_call(
        lambda *refs: fields_kernel(devices, *refs),
        out_shape=(
            jax.ShapeDtypeStruct((devices, walk_total, chol_local), jnp.bfloat16),
            jax.ShapeDtypeStruct((walk_total, 128), jnp.float32),
        ),
        in_specs=[VMEM, VMEM],
        out_specs=(VMEM, VMEM),
        scratch_shapes=[
            pltpu.VMEM((devices, walk_total, chol_local), jnp.float32),
            pltpu.VMEM((walk_total, chol_local), jnp.bfloat16),
            pltpu.VMEM((walk_total, 128), jnp.float32),
            pltpu.VMEM((devices, walk_total, 128), jnp.float32),
        ] + [sems] * 6,
        compiler_params=pltpu.CompilerParams(collective_id=1, has_side_effects=True),
        name="fields",
    )(partial_bias, noise)


def density(orbital_matrix):
    intersection = jnp.dot(orbital_matrix, orbital_matrix.T, precision=lax.Precision.HIGHEST)
    factor = jnp.linalg.cholesky(intersection)
    rotated = lax.linalg.triangular_solve(factor, orbital_matrix, left_side=True, lower=True)
    return jnp.dot(rotated.T, rotated, precision=lax.Precision.HIGHEST)


def gaussian(seed_values):
    first = (seed_values % 65521 * 7919 + 13) % 65521
    second = (seed_values // 2 * 3037 + 101) % 65521
    uniform_one = (first.astype(jnp.float32) + 0.5) / 65521.0
    uniform_two = (second.astype(jnp.float32) + 0.5) / 65521.0
    return jnp.sqrt(-2.0 * jnp.log(uniform_one)) * jnp.cos(2.0 * math.pi * uniform_two)


def per_device(walkers, cholesky, field_seeds, slot_order):
    walk_local = walkers.shape[0]
    orbits = walkers.shape[2]
    halfway = orbits // 2
    devices = lax.axis_size("pair")
    own_index = lax.axis_index("pair")
    chol_total = cholesky.shape[0]
    rows_local = cholesky.shape[1]
    row_width = cholesky.shape[2]
    chol_local = chol_total // devices
    walk_total = walk_local * devices
    noise = gaussian(field_seeds[:, slot_order]).T
    greens = jax.vmap(density)(walkers).astype(jnp.bfloat16)
    folded = jnp.stack([fold(greens[w]) for w in range(walk_local)], axis=0)
    blocks = folded.reshape(walk_local, devices, rows_local, row_width).swapaxes(0, 1)
    packed = exchange(blocks, devices, 0, "density_out").reshape(
        walk_total, rows_local, row_width
    )
    partial_bias = lax.dot_general(
        cholesky, packed, (((1, 2), (1, 2)), ((), ())), preferred_element_type=jnp.float32
    ).T
    partial_bias = partial_bias.reshape(walk_total, devices, chol_local).swapaxes(0, 1)
    all_shifted, log_total = fields(partial_bias, noise, devices)
    shifted = all_shifted.swapaxes(0, 1).reshape(walk_total, chol_total)
    potential = sqrt_step * lax.dot_general(
        shifted, cholesky, (((1,), (0,)), ((), ())), preferred_element_type=jnp.float32
    )
    outgoing = potential.astype(jnp.bfloat16).reshape(
        devices, walk_local, rows_local, row_width
    )
    returned = exchange(outgoing, devices, 2, "potential_back")
    own_potential = returned.swapaxes(0, 1).reshape(walk_local, halfway, row_width)
    moved = jnp.stack(
        [propagate(own_potential[w], walkers[w]) for w in range(walk_local)], axis=0
    )
    own_log = lax.dynamic_slice_in_dim(log_total[:, 0], own_index * walk_local, walk_local, 0)
    return (moved, own_log)


def solution(mesh):
    return jax.shard_map(
        per_device,
        mesh=mesh,
        in_specs=(
            P(("geom", "pair"), None, None),
            P("geom", "pair", None),
            P("pair", "geom"),
            P("geom"),
        ),
        out_specs=(P(("geom", "pair"), None, None), P(("geom", "pair"))),
        check_vma=False,
    )
```

```python
import math

import jax
import jax.numpy as jnp
from jax import lax
from jax.experimental import pallas as pl
from jax.experimental.pallas import tpu as pltpu
from jax.sharding import PartitionSpec as P

sqrt_step = 0.1
VMEM = pl.BlockSpec(memory_space=pltpu.VMEM)


def flip_matrix(size):
    row = lax.broadcasted_iota(jnp.int32, (size, size), 0)
    col = lax.broadcasted_iota(jnp.int32, (size, size), 1)
    return jnp.where(row + col == size - 1, 1.0, 0.0).astype(jnp.bfloat16)


def exact_dot(a, b):
    return jnp.dot(a, b, preferred_element_type=jnp.float32)


def fold_kernel(green_ref, out_ref):
    orbits = green_ref.shape[0]
    halfway = orbits // 2
    flip_half = flip_matrix(halfway)
    upper = exact_dot(flip_half, green_ref[:halfway, :])
    lower = exact_dot(green_ref[halfway:, :], flip_matrix(orbits))
    joined = jnp.concatenate([upper, lower], axis=1)
    rolled = pltpu.roll(joined, orbits + halfway + 1, 1, stride=1, stride_axis=0)
    column = lax.broadcasted_iota(jnp.int32, (halfway, 2 * orbits), 1)
    weighted = jnp.where((column == 0) | (column == orbits), rolled, 2.0 * rolled)
    ordered = exact_dot(flip_half, weighted.astype(jnp.bfloat16))
    out_ref[...] = ordered[:, : orbits + 1].astype(jnp.bfloat16)


def fold(green):
    orbits = green.shape[0]
    return pl.pallas_call(
        fold_kernel,
        out_shape=jax.ShapeDtypeStruct((orbits // 2, orbits + 1), jnp.bfloat16),
        in_specs=[VMEM],
        out_specs=VMEM,
        name="fold",
    )(green)


def propagate_kernel(packed_ref, orbital_ref, out_ref):
    halfway, width = packed_ref.shape
    orbits = width - 1
    packed = packed_ref[...].astype(jnp.float32)
    padded = jnp.concatenate(
        [packed, jnp.zeros((halfway, 2 * orbits - width), jnp.float32)], axis=1
    )
    spread = pltpu.roll(padded, 0, 1, stride=1, stride_axis=0)
    backward = spread[:, orbits:].astype(jnp.bfloat16)
    turned = exact_dot(flip_matrix(halfway), backward).astype(jnp.bfloat16)
    lower = exact_dot(turned, flip_matrix(orbits))
    upper = jnp.concatenate([spread[:, :orbits], lower], axis=0)
    row = lax.broadcasted_iota(jnp.int32, (orbits, orbits), 0)
    col = lax.broadcasted_iota(jnp.int32, (orbits, orbits), 1)
    potential = jnp.where(col >= row, upper, upper.T).astype(jnp.bfloat16)
    term = orbital_ref[...]
    count = term.shape[0]
    result = term
    for degree in range(1, 7):
        high = term.astype(jnp.bfloat16)
        rest = term - high.astype(jnp.float32)
        middle = rest.astype(jnp.bfloat16)
        low = (rest - middle.astype(jnp.float32)).astype(jnp.bfloat16)
        product = exact_dot(jnp.concatenate([high, middle, low], axis=0), potential)
        term = (
            product[2 * count :] + product[count : 2 * count] + product[:count]
        ) * (1.0 / degree)
        result = result + term
    out_ref[...] = result


def propagate(packed_potential, orbital_matrix):
    return pl.pallas_call(
        propagate_kernel,
        out_shape=jax.ShapeDtypeStruct(orbital_matrix.shape, jnp.float32),
        in_specs=[VMEM, VMEM],
        out_specs=VMEM,
        name="propagate",
    )(packed_potential, orbital_matrix)


def meet_everyone(devices, own):
    barrier = pltpu.get_barrier_semaphore()

    def greet(step, carry):
        peer = lax.rem(own + step, devices)
        pl.semaphore_signal(
            barrier, inc=1, device_id={"pair": peer}, device_id_type=pl.DeviceIdType.MESH
        )
        return carry

    lax.fori_loop(1, devices, greet, 0)
    pl.semaphore_wait(barrier, devices - 1)


def remote(source, target, send_sem, recv_sem, step, peer):
    return pltpu.make_async_remote_copy(
        src_ref=source,
        dst_ref=target,
        send_sem=send_sem.at[step],
        recv_sem=recv_sem.at[step],
        device_id={"pair": peer},
        device_id_type=pl.DeviceIdType.MESH,
    )


def exchange_kernel(devices, in_ref, out_ref, send_sem, recv_sem, local_sem):
    own = lax.axis_index("pair")
    local = pltpu.make_async_copy(in_ref.at[own], out_ref.at[own], local_sem)
    local.start()
    meet_everyone(devices, own)

    def start(step, carry):
        peer = lax.rem(own + step, devices)
        remote(in_ref.at[peer], out_ref.at[own], send_sem, recv_sem, step, peer).start()
        return carry

    def finish(step, carry):
        peer = lax.rem(own + step, devices)
        source = lax.rem(own + devices - step, devices)
        remote(in_ref.at[peer], out_ref.at[source], send_sem, recv_sem, step, peer).wait()
        return carry

    lax.fori_loop(1, devices, start, 0)
    lax.fori_loop(1, devices, finish, 0)
    local.wait()


def exchange(blocks, devices, collective_id, name):
    return pl.pallas_call(
        lambda *refs: exchange_kernel(devices, *refs),
        out_shape=jax.ShapeDtypeStruct(blocks.shape, blocks.dtype),
        in_specs=[VMEM],
        out_specs=VMEM,
        scratch_shapes=[
            pltpu.SemaphoreType.DMA((devices,)),
            pltpu.SemaphoreType.DMA((devices,)),
            pltpu.SemaphoreType.DMA,
        ],
        compiler_params=pltpu.CompilerParams(
            collective_id=collective_id, has_side_effects=True
        ),
        name=name,
    )(blocks)


def fields_kernel(
    devices, partial_ref, noise_ref, shifted_ref, log_ref,
    arrived, own_shifted, own_log, all_log,
    bias_send, bias_recv, field_send, field_recv, log_send, log_recv,
):
    own = lax.axis_index("pair")
    meet_everyone(devices, own)

    def bias_copy(step, slot):
        peer = lax.rem(own + step, devices)
        return remote(partial_ref.at[peer], arrived.at[slot], bias_send, bias_recv, step, peer)

    def field_copy(step, slot):
        peer = lax.rem(own + step, devices)
        return remote(own_shifted, shifted_ref.at[slot], field_send, field_recv, step, peer)

    def log_copy(step, slot):
        peer = lax.rem(own + step, devices)
        return remote(own_log.at[peer], all_log.at[slot], log_send, log_recv, step, peer)

    def start_bias(step, carry):
        bias_copy(step, own).start()
        return carry

    def finish_bias(step, total):
        source = lax.rem(own + devices - step, devices)
        bias_copy(step, source).wait()
        return total + arrived[source]

    lax.fori_loop(1, devices, start_bias, 0)
    bias = sqrt_step * lax.fori_loop(1, devices, finish_bias, partial_ref[own])
    noise = noise_ref[...]
    shifted = (noise - bias).astype(jnp.bfloat16)
    own_shifted[...] = shifted
    terms = jnp.sum(noise * bias - 0.5 * bias * bias, axis=1, keepdims=True)
    own_log[...] = jnp.broadcast_to(terms[:, :, None].reshape(own_log.shape[:2] + (1,)), own_log.shape)

    def start_fields(step, carry):
        field_copy(step, own).start()
        return carry

    def start_logs(step, carry):
        log_copy(step, own).start()
        return carry

    def finish_fields(step, carry):
        source = lax.rem(own + devices - step, devices)
        field_copy(step, source).wait()
        return carry

    def finish_logs(step, total):
        source = lax.rem(own + devices - step, devices)
        log_copy(step, source).wait()
        return total + all_log[source]

    lax.fori_loop(1, devices, start_fields, 0)
    lax.fori_loop(1, devices, start_logs, 0)
    shifted_ref[own] = shifted
    lax.fori_loop(1, devices, finish_fields, 0)
    log_ref[...] = lax.fori_loop(1, devices, finish_logs, own_log[own])


def fields(partial_bias, noise, devices):
    walk_total, chol_local = noise.shape
    walk_local = walk_total // devices
    sems = pltpu.SemaphoreType.DMA((devices,))
    return pl.pallas_call(
        lambda *refs: fields_kernel(devices, *refs),
        out_shape=(
            jax.ShapeDtypeStruct((devices, walk_total, chol_local), jnp.bfloat16),
            jax.ShapeDtypeStruct((walk_local, 128), jnp.float32),
        ),
        in_specs=[VMEM, VMEM],
        out_specs=(VMEM, VMEM),
        scratch_shapes=[
            pltpu.VMEM((devices, walk_total, chol_local), jnp.float32),
            pltpu.VMEM((walk_total, chol_local), jnp.bfloat16),
            pltpu.VMEM((devices, walk_local, 128), jnp.float32),
            pltpu.VMEM((devices, walk_local, 128), jnp.float32),
        ] + [sems] * 6,
        compiler_params=pltpu.CompilerParams(collective_id=1, has_side_effects=True),
        name="fields",
    )(partial_bias, noise)


def density(orbital_matrix):
    intersection = jnp.dot(orbital_matrix, orbital_matrix.T, precision=lax.Precision.HIGHEST)
    factor = jnp.linalg.cholesky(intersection)
    rotated = lax.linalg.triangular_solve(factor, orbital_matrix, left_side=True, lower=True)
    return jnp.dot(rotated.T, rotated, precision=lax.Precision.HIGHEST)


def gaussian(seed_values):
    first = (seed_values % 65521 * 7919 + 13) % 65521
    second = (seed_values // 2 * 3037 + 101) % 65521
    uniform_one = (first.astype(jnp.float32) + 0.5) / 65521.0
    uniform_two = (second.astype(jnp.float32) + 0.5) / 65521.0
    return jnp.sqrt(-2.0 * jnp.log(uniform_one)) * jnp.cos(2.0 * math.pi * uniform_two)


def per_device(walkers, cholesky, field_seeds, slot_order):
    walk_local = walkers.shape[0]
    orbits = walkers.shape[2]
    halfway = orbits // 2
    devices = lax.axis_size("pair")
    chol_total = cholesky.shape[0]
    rows_local = cholesky.shape[1]
    row_width = cholesky.shape[2]
    chol_local = chol_total // devices
    walk_total = walk_local * devices
    noise = gaussian(field_seeds[:, slot_order]).T
    greens = jax.vmap(density)(walkers).astype(jnp.bfloat16)
    folded = jnp.stack([fold(greens[w]) for w in range(walk_local)], axis=0)
    blocks = folded.reshape(walk_local, devices, rows_local, row_width).swapaxes(0, 1)
    packed = exchange(blocks, devices, 0, "density_out").reshape(
        walk_total, rows_local, row_width
    )
    flat_packed = packed.transpose(0, 2, 1).reshape(walk_total, row_width * rows_local)
    flat_chol = cholesky.transpose(2, 1, 0).reshape(row_width * rows_local, chol_total)
    partial_bias = lax.optimization_barrier(
        jnp.dot(flat_packed, flat_chol, preferred_element_type=jnp.float32)
    )
    partial_bias = partial_bias.reshape(walk_total, devices, chol_local).swapaxes(0, 1)
    all_shifted, log_total = fields(partial_bias, noise, devices)
    shifted = all_shifted.swapaxes(0, 1).reshape(walk_total, chol_total)
    potential = sqrt_step * lax.dot_general(
        shifted, flat_chol, (((1,), (1,)), ((), ())), preferred_element_type=jnp.float32
    )
    potential = lax.optimization_barrier(potential.astype(jnp.bfloat16))
    outgoing = (
        potential.reshape(walk_total, row_width, rows_local)
        .transpose(0, 2, 1)
        .reshape(devices, walk_local, rows_local, row_width)
    )
    returned = exchange(outgoing, devices, 2, "potential_back")
    own_potential = returned.swapaxes(0, 1).reshape(walk_local, halfway, row_width)
    moved = jnp.stack(
        [propagate(own_potential[w], walkers[w]) for w in range(walk_local)], axis=0
    )
    return (moved, log_total[:, 0])


def solution(mesh):
    return jax.shard_map(
        per_device,
        mesh=mesh,
        in_specs=(
            P(("geom", "pair"), None, None),
            P("geom", "pair", None),
            P("pair", "geom"),
            P("geom"),
        ),
        out_specs=(P(("geom", "pair"), None, None), P(("geom", "pair"))),
        check_vma=False,
    )
```
